32 devices in a mesh: ctx: 8 (over y, x, core), dp: 4 (over z).
Axes of the slice: x: 2, y: 2, z: 4, core: 2. Of those that a mesh axis runs over, the one named last changes fastest.
Arguments:
- ids: int32 [3072], P('ctx'), may hold values from 0 to 511
- embed_table: bfloat16 [512, 4096], P(None, 'dp'), may hold values from -6 to 6
- norm_gain: bfloat16 [4096], P('dp'), may hold values from 0.25 to 1.75
- w_query: bfloat16 [4096, 4096], P('ctx', 'dp'), may hold values from -0.09375 to 0.09375
- w_key: bfloat16 [4096, 4096], P('ctx', 'dp'), may hold values from -0.09375 to 0.09375
- w_value: bfloat16 [4096, 4096], P('ctx', 'dp'), may hold values from -0.09375 to 0.09375
- short_filter: float32 [3, 3, 4096], P(None, None, 'dp'), may hold values from -4 to 4
- pole_rate: float32 [4096, 16], P('dp'), may hold values from 1.6276042e-05 to 0.05
- residue: float32 [4096, 16], P('dp'), may hold values from -2 to 2
- skip_gain: float32 [4096], P('dp'), may hold values from -4 to 4
- w_out: bfloat16 [4096, 4096], P('ctx', 'dp'), may hold values from -0.09375 to 0.09375
Outputs:
- block_out: bfloat16 [3072, 4096], P('ctx', 'dp')
The draws below stay inside these ranges and needn't reach their ends.
All inputs are finite; a program needn't handle non-finite values.
Results may differ from the reference program's by a relative error of at most 0.0082.
Values may be sent and summed in bfloat16 or wider, within the bound.
A program may use at most 128 MiB of HBM per device.

```python
import math
import jax
import jax.numpy as jnp
import numpy as np
from jax import lax

D = 4096
VOCAB = 512
MODES = 16
TAPS = 3
TOKENS = 3072


def draw_pole_rate(key, part):
    key_pick = jax.random.fold_in(key, 11)
    key_fast = jax.random.fold_in(key, 12)
    key_slow = jax.random.fold_in(key, 13)
    selector = jax.random.uniform(key_pick, (D, MODES), jnp.float32)
    fast_rates = jnp.exp(jax.random.uniform(key_fast, (D, MODES), jnp.float32, math.log(0.02), math.log(0.05)))
    slow_rates = jnp.exp(jax.random.uniform(key_slow, (D, MODES), jnp.float32, math.log(0.05), math.log(2.0))) / TOKENS
    share_fast = 0.5
    return jnp.where(selector < share_fast, fast_rates, slow_rates)


def with_ends(array, key, least, top_value):
    extent = array.shape
    spot = [jax.random.randint(jax.random.fold_in(key, axis), (), 0, extent[axis]) for axis in range(len(extent))]
    array = array.at[tuple(spot)].set(least)
    longest = extent.index(max(extent))
    spot[longest] = (spot[longest] + 1) % extent[longest]
    return array.at[tuple(spot)].set(top_value)


def shard_levels(key, dims, shards, least, top_value):
    gain, own = 1.0, jax.random.fold_in(key, 6)
    for axis_at, blocks in shards:
        steps = jnp.exp(jax.random.uniform(jax.random.fold_in(own, axis_at), (blocks,), jnp.float32, least / len(shards), top_value / len(shards)))
        gain = gain * jnp.repeat(steps, dims[axis_at] // blocks).reshape([-1 if axis == axis_at else 1 for axis in range(len(dims))])
    return gain


def cumulative_ranks(count, skew):
    loads = [(1 << 20) // math.isqrt(grade ** skew) + 1 for grade in range(1, count + 1)]
    width = 1 + sum(loads) // (1 << 30)
    return np.cumsum(np.array([max(1, weight // width) for weight in loads]))


def ranked_ids(stream_key, extent, amount, lean):
    grid = cumulative_ranks(amount, lean)
    pick = jax.random.randint(jax.random.fold_in(stream_key, 1), extent, 0, int(grid[amount - 1]))
    grade = jnp.searchsorted(jnp.asarray(grid, jnp.int32), pick, side="right")
    return jax.random.permutation(jax.random.fold_in(stream_key, 2), amount)[grade].astype(jnp.int32)


def gaussian(key, shape, deviation, bound, split=(), held_as=jnp.bfloat16):
    result = jax.random.normal(key, shape, jnp.float32) * deviation
    if len(split) > 0:
        result = shard_levels(key, shape, split, -0.22, 0.18) * result
    return jnp.clip(result, min=-bound, max=bound).astype(held_as)


def setup_inputs(seed: int = 0) -> dict:
    arg_keys = jax.random.split(jax.random.key(seed), 12)
    return {
        "ids": with_ends(ranked_ids(arg_keys[0], (TOKENS,), VOCAB, 2), jax.random.fold_in(arg_keys[0], 3), 0, VOCAB - 1).astype(jnp.int32),
        "embed_table": gaussian(arg_keys[1], (VOCAB, D), 1.0, 6.0, ((1, 4),)),
        "norm_gain": jnp.clip(1.0 + 0.15 * jax.random.normal(arg_keys[2], (D,), jnp.float32), 0.25, 1.75).astype(jnp.bfloat16),
        "w_query": gaussian(arg_keys[3], (D, D), D ** -0.5, 0.09375, ((0, 8), (1, 4))),
        "w_key": gaussian(arg_keys[4], (D, D), D ** -0.5, 0.09375, ((0, 8), (1, 4))),
        "w_value": gaussian(arg_keys[5], (D, D), D ** -0.5, 0.09375, ((0, 8), (1, 4))),
        "short_filter": gaussian(arg_keys[6], (TAPS, 3, D), 0.6, 4.0, ((2, 4),), jnp.float32),
        "pole_rate": draw_pole_rate(jax.random.fold_in(arg_keys[11], 71), 0),
        "residue": gaussian(arg_keys[8], (D, MODES), 0.3, 2.0, ((0, 4),), jnp.float32),
        "skip_gain": gaussian(arg_keys[9], (D,), 1.0, 4.0, ((0, 4),), jnp.float32),
        "w_out": gaussian(arg_keys[10], (D, D), D ** -0.5, 0.09375, ((0, 8), (1, 4))),
    }


def reference(ids, embed_table, norm_gain, w_query, w_key, w_value, short_filter, pole_rate, residue, skip_gain, w_out):
    embedded = embed_table[ids]
    floated = embedded.astype(jnp.float32)
    scale = lax.rsqrt(lax.optimization_barrier(jnp.mean(floated * floated, axis=1, keepdims=True)) + 1e-06)
    normed = (floated * scale * norm_gain.astype(jnp.float32)[None, :]).astype(jnp.bfloat16)
    convs = []
    for index, weight in enumerate((w_query, w_key, w_value)):
        proj = jnp.dot(normed, weight, preferred_element_type=jnp.float32).astype(jnp.bfloat16)
        padded = jnp.pad(proj.astype(jnp.float32), ((TAPS - 1, 0), (0, 0)))
        conv = jnp.zeros((TOKENS, D), jnp.float32)
        for tap in range(TAPS):
            conv = conv + short_filter[tap, index][None, :] * padded[TAPS - 1 - tap:TAPS - 1 - tap + TOKENS]
        convs.append(conv)
    query_conv, key_conv, value_conv = convs
    gated = key_conv * value_conv
    decay = jnp.exp(-pole_rate)
    strength = residue * jnp.sqrt(2.0 * pole_rate)

    def advance(state, row):
        state = decay * state + row[:, None]
        return (state, lax.optimization_barrier(jnp.sum(strength * state, axis=1)))
    final_state, filtered = lax.scan(advance, jnp.zeros((D, MODES), jnp.float32), gated)
    long_conv = filtered + skip_gain[None, :] * gated
    mixed = (query_conv * long_conv).astype(jnp.bfloat16)
    output = jnp.dot(mixed, w_out, preferred_element_type=jnp.float32)
    return (floated + output).astype(jnp.bfloat16)
```

```python
import math

import jax
import jax.numpy as jnp
from jax import lax

from jax.experimental import pallas as pl
from jax.experimental.pallas import tpu as pltpu
from jax.sharding import PartitionSpec as P

MESH = pl.DeviceIdType.MESH
LANES = 128
SUBLANES = 8
VMEM_BYTES = 56 << 20


def shifted(value, axis, steps):
    count = lax.axis_size(axis)
    initial, last = (max(0, -steps), min(count, count - steps))
    return lax.ppermute(value, axis, [(source, source + steps) for source in range(initial, last)])


def entering_2(value, axis, combine, identity):
    peers, index = (lax.axis_size(axis), lax.axis_index(axis))
    everything = jax.tree.map(lambda part: lax.all_gather(part, axis), value)
    start = jax.tree.map(
        lambda part, zero: jnp.broadcast_to(jnp.asarray(zero, part.dtype), part.shape),
        value,
        identity,
    )

    def turn(k, before):
        reached = k < index
        new = combine(before, jax.tree.map(lambda part: part[k], everything))
        return jax.tree.map(lambda a, b: jnp.where(reached, a, b), new, before)

    return lax.fori_loop(0, peers, turn, start)


def shards(
    ids,
    embed_table,
    norm_gain,
    w_query,
    w_key,
    w_value,
    short_filter,
    pole_rate,
    residue,
    skip_gain,
    w_out,
):
    highest = lax.Precision.HIGHEST
    vocab = embed_table.shape[0]
    channels = w_query.shape[1]
    one_hot = (ids[:, None] == jnp.arange(vocab, dtype=jnp.int32)[None, :]).astype(jnp.bfloat16)
    embedded = jnp.dot(one_hot, embed_table, preferred_element_type=jnp.float32).astype(
        jnp.bfloat16
    )
    full_rows, full_gain = (
        lax.all_gather(embedded, "dp", axis=1, tiled=True),
        lax.all_gather(norm_gain, "dp", axis=0, tiled=True),
    )
    floated = full_rows.astype(jnp.float32)
    scale = lax.rsqrt(jnp.mean(floated * floated, axis=1, keepdims=True) + 1e-06)
    normed = (floated * scale * full_gain.astype(jnp.float32)[None, :]).astype(jnp.bfloat16)
    tok_rows = normed.shape[0]

    def add_rows(piece):
        return jnp.dot(normed, piece, preferred_element_type=jnp.float32)

    query_proj = add_rows(lax.all_gather(w_query, "ctx", axis=0, tiled=True))
    key_proj = add_rows(lax.all_gather(w_key, "ctx", axis=0, tiled=True))
    value_proj = add_rows(lax.all_gather(w_value, "ctx", axis=0, tiled=True))
    projected = jnp.concatenate([query_proj, key_proj, value_proj], axis=1).astype(jnp.bfloat16)
    taps = short_filter.shape[0]
    previous = shifted(projected[tok_rows - (taps - 1) :], "ctx", 1)
    extended = jnp.concatenate([previous, projected], axis=0).astype(jnp.float32)
    filt_rows = short_filter.reshape(taps, 3 * channels)
    convolved = jnp.zeros((tok_rows, 3 * channels), jnp.float32)
    for tap in range(taps):
        convolved = (
            convolved
            + filt_rows[tap][None, :] * extended[taps - 1 - tap : taps - 1 - tap + tok_rows]
        )
    query_conv = convolved[:, :channels]
    gated = convolved[:, channels : 2 * channels] * convolved[:, 2 * channels :]
    sub_len = math.gcd(tok_rows, 64)
    blocks = tok_rows // sub_len
    lag_index = jnp.arange(sub_len, dtype=jnp.int32)
    lags = lag_index.astype(jnp.float32)
    strength = residue * jnp.sqrt(2.0 * pole_rate)
    kernel = jnp.einsum(
        "lck,ck->lc", jnp.exp(-pole_rate[None] * lags[:, None, None]), strength, precision=highest
    )
    offsets = lag_index[:, None] - lag_index[None, :]
    toeplitz = jnp.where((offsets >= 0)[:, :, None], kernel[jnp.maximum(offsets, 0)], 0.0)
    pieces = gated.reshape(blocks, sub_len, channels)
    inside = jnp.einsum("tsc,bsc->btc", toeplitz, pieces, precision=highest)
    tail_decay = jnp.exp(-pole_rate[None] * (sub_len - 1.0 - lags)[:, None, None])
    block_ends = jnp.einsum("sck,bsc->bck", tail_decay, pieces, precision=highest)
    step_decay = jnp.exp(-pole_rate * float(sub_len))

    def advance(state, block_end):
        return (step_decay * state + block_end, state)

    device_end, entering = lax.scan(advance, jnp.zeros_like(step_decay), block_ends)
    device_decay = jnp.exp(-pole_rate * float(tok_rows))

    def combine(earlier, later):
        return (earlier[0] * later[0], later[0] * earlier[1] + later[1])

    decay_total, incoming = entering_2(
        (device_decay, device_end),
        "ctx",
        combine,
        (jnp.ones_like(device_decay), jnp.zeros_like(device_end)),
    )
    block_pos = jnp.arange(blocks, dtype=jnp.float32) * float(sub_len)
    states_in = entering + jnp.exp(-pole_rate[None] * block_pos[:, None, None]) * incoming[None]
    lead = jnp.exp(-pole_rate[None] * (lags + 1.0)[:, None, None]) * strength[None]
    carried = jnp.einsum("tck,bck->btc", lead, states_in, precision=highest)
    long_conv = (inside + carried).reshape(tok_rows, channels) + skip_gain[None, :] * gated
    mixed = (query_conv * long_conv).astype(jnp.bfloat16)
    all_mixed = lax.all_gather(mixed, "dp", axis=1, tiled=True)
    output = jnp.dot(
        all_mixed,
        lax.all_gather(w_out, "ctx", axis=0, tiled=True),
        preferred_element_type=jnp.float32,
    )
    return (embedded.astype(jnp.float32) + output).astype(jnp.bfloat16)


def remote(src, dst, send, recv, **where):
    return pltpu.make_async_remote_copy(
        src_ref=src,
        dst_ref=dst,
        send_sem=send,
        recv_sem=recv,
        device_id=where,
        device_id_type=MESH,
    )


def greet(ctx_peers, dp_peers):
    barrier = pltpu.get_barrier_semaphore()
    for peer in ctx_peers:
        pl.semaphore_signal(barrier, inc=1, device_id={"ctx": peer}, device_id_type=MESH)
    for peer in dp_peers:
        pl.semaphore_signal(barrier, inc=1, device_id={"dp": peer}, device_id_type=MESH)
    pl.semaphore_wait(barrier, len(ctx_peers) + len(dp_peers))


def flip(index, bit):
    return index + bit - 2 * bit * (lax.rem(index // bit, 2))


def spread_kernel(
    n_ctx,
    n_dp,
    ids_ref,
    gain_ref,
    table_ref,
    wq_ref,
    wk_ref,
    wv_ref,
    ids_out,
    gain_out,
    table_out,
    w_out,
    own_w,
    own_table,
    w_send,
    w_recv,
    id_send,
    id_recv,
    gain_send,
    gain_recv,
    z_send,
    z_recv,
    core_send,
    core_recv,
    local,
):
    me, at = lax.axis_index("ctx"), lax.axis_index("dp")
    depth, wide = wq_ref.shape[0], wq_ref.shape[1] // n_ctx
    vocab = table_ref.shape[0]
    chunks = z_send.shape[2]
    part = vocab // 2 // chunks
    partner = flip(me, 1)
    ctx_peers = [lax.rem(me + d, n_ctx) for d in range(1, n_ctx)]
    dp_peers = [lax.rem(at + d, n_dp) for d in range(1, n_dp)]
    greet(ctx_peers, dp_peers)
    rows = pl.ds(pl.multiple_of(me * depth, depth), depth)
    weights = (wq_ref, wk_ref, wv_ref)

    def half_chunk(core, k):
        return pl.ds(pl.multiple_of((core * chunks + k) * part, part), part)

    def z_copy(source, k, way, hop, peer):
        piece = half_chunk(lax.rem(me, 2), k)
        src = table_ref.at[piece] if hop == 0 else table_out.at[source, piece]
        return remote(
            src,
            table_out.at[source, piece],
            z_send.at[way, hop, k],
            z_recv.at[source, k],
            dp=peer,
        )

    def core_copy(source, core, k):
        piece = half_chunk(core, k)
        return remote(
            table_out.at[source, piece],
            table_out.at[source, piece],
            core_send.at[source, k],
            core_recv.at[source, k],
            ctx=partner,
        )

    for k in range(chunks):

        @pl.when(at < n_dp - 1)
        def _():
            z_copy(at, k, 0, 0, at + 1).start()

        @pl.when(at > 0)
        def _():
            z_copy(at, k, 1, 0, at - 1).start()

    sends = []
    for d, peer in enumerate(ctx_peers):
        copy = remote(ids_ref, ids_out.at[me], id_send.at[d], id_recv.at[me], ctx=peer)
        copy.start()
        sends.append(copy)
    for d, peer in enumerate(dp_peers):
        copy = remote(gain_ref, gain_out.at[at], gain_send.at[d], gain_recv.at[at], dp=peer)
        copy.start()
        sends.append(copy)
    for d, peer in enumerate(ctx_peers):
        for w, weight in enumerate(weights):
            copy = remote(
                weight.at[:, pl.ds(pl.multiple_of(peer * wide, wide), wide)],
                w_out.at[rows, pl.ds(w * wide, wide)],
                w_send.at[d, w],
                w_recv.at[me, w],
                ctx=peer,
            )
            copy.start()
            sends.append(copy)
    into = [
        pltpu.make_async_copy(
            weight.at[:, pl.ds(pl.multiple_of(me * wide, wide), wide)],
            own_w.at[:, pl.ds(w * wide, wide)],
            local.at[w],
        )
        for w, weight in enumerate(weights)
    ]
    into.append(pltpu.make_async_copy(table_ref, own_table, local.at[3]))
    into.append(pltpu.make_async_copy(ids_ref, ids_out.at[me], local.at[4]))
    into.append(pltpu.make_async_copy(gain_ref, gain_out.at[at], local.at[5]))
    for copy in into:
        copy.start()
    for copy in into:
        copy.wait()
    out = [
        pltpu.make_async_copy(own_w, w_out.at[rows], local.at[0]),
        pltpu.make_async_copy(own_table, table_out.at[at], local.at[1]),
    ]
    for copy in out:
        copy.start()

    core = lax.rem(me, 2)
    for hop in range(1, n_dp):
        for k in range(chunks):

            @pl.when(at - hop >= 0)
            def _():
                z_copy(at - hop, k, 0, 0, at).wait_recv()
                core_copy(at - hop, core, k).start()

                if hop < n_dp - 1:

                    @pl.when(at < n_dp - 1)
                    def _():
                        z_copy(at - hop, k, 0, hop, at + 1).start()

            @pl.when(at + hop <= n_dp - 1)
            def _():
                z_copy(at + hop, k, 1, 0, at).wait_recv()
                core_copy(at + hop, core, k).start()

                if hop < n_dp - 1:

                    @pl.when(at > 0)
                    def _():
                        z_copy(at + hop, k, 1, hop, at - 1).start()

    for d in range(1, n_dp):
        source = lax.rem(at + d, n_dp)
        for k in range(chunks):
            core_copy(source, 1 - core, k).wait_recv()
            core_copy(source, core, k).wait_send()
    for hop in range(n_dp - 1):
        for k in range(chunks):

            @pl.when((at - hop >= 0) & (at < n_dp - 1))
            def _():
                z_copy(at - hop, k, 0, hop, at + 1).wait_send()

            @pl.when((at + hop <= n_dp - 1) & (at > 0))
            def _():
                z_copy(at + hop, k, 1, hop, at - 1).wait_send()

    for d, peer in enumerate(ctx_peers):
        remote(ids_ref, ids_out.at[peer], id_send.at[d], id_recv.at[peer], ctx=peer).wait_recv()
        theirs = pl.ds(pl.multiple_of(peer * depth, depth), depth)
        for w, weight in enumerate(weights):
            remote(
                weight.at[:, pl.ds(pl.multiple_of(peer * wide, wide), wide)],
                w_out.at[theirs, pl.ds(w * wide, wide)],
                w_send.at[d, w],
                w_recv.at[peer, w],
                ctx=peer,
            ).wait_recv()
    for d, peer in enumerate(dp_peers):
        remote(gain_ref, gain_out.at[peer], gain_send.at[d], gain_recv.at[peer], dp=peer).wait_recv()
    for copy in sends:
        copy.wait_send()
    for copy in out:
        copy.wait()


def spread(n_ctx, n_dp, ids, gain, table, w_query, w_key, w_value):
    depth, wide = w_query.shape[0], w_query.shape[1] // n_ctx
    chunks = 2
    anywhere = pl.BlockSpec(memory_space=pl.ANY)
    dma = pltpu.SemaphoreType.DMA
    return pl.pallas_call(
        lambda *refs: spread_kernel(n_ctx, n_dp, *refs),
        name="spread",
        out_shape=(
            jax.ShapeDtypeStruct((n_ctx, *ids.shape), ids.dtype),
            jax.ShapeDtypeStruct((n_dp, *gain.shape), gain.dtype),
            jax.ShapeDtypeStruct((n_dp, *table.shape), table.dtype),
            jax.ShapeDtypeStruct((n_ctx * depth, 3 * wide), w_query.dtype),
        ),
        in_specs=[anywhere] * 6,
        out_specs=[anywhere] * 4,
        scratch_shapes=[
            pltpu.VMEM((depth, 3 * wide), w_query.dtype),
            pltpu.VMEM(table.shape, table.dtype),
            dma((n_ctx - 1, 3)),
            dma((n_ctx, 3)),
            dma((n_ctx - 1,)),
            dma((n_ctx,)),
            dma((n_dp - 1,)),
            dma((n_dp,)),
            dma((2, n_dp - 1, chunks)),
            dma((n_dp, chunks)),
            dma((n_dp, chunks)),
            dma((n_dp, chunks)),
            dma((6,)),
        ],
        compiler_params=pltpu.CompilerParams(
            collective_id=0, has_side_effects=True, vmem_limit_bytes=8 << 20
        ),
    )(ids, gain, table, w_query, w_key, w_value)


def mix_kernel(
    ids_ref,
    gain_ref,
    table_ref,
    w_ref,
    filt_ref,
    rate_ref,
    residue_ref,
    skip_ref,
    out_ref,
    proj,
    gated,
    query,
):
    n_dp, vocab, width = table_ref.shape
    features = n_dp * width
    taps = filt_ref.shape[0]
    modes = rate_ref.shape[0]
    segments, steps, lanes = out_ref.shape
    lead = proj.shape[0] - segments * steps
    total = jnp.zeros((vocab, 1), jnp.float32)
    for b in range(n_dp):
        block = table_ref[b].astype(jnp.float32)
        total = total + jnp.sum(block * block, axis=1, keepdims=True)
    scale = lax.rsqrt(total / features + 1e-06)
    rows = jnp.zeros((vocab, 3 * lanes), jnp.float32)
    for b in range(n_dp):
        block = table_ref[b].astype(jnp.float32)
        normed = (block * scale * gain_ref[:, b * width : (b + 1) * width]).astype(jnp.bfloat16)
        rows = rows + jnp.dot(
            normed, w_ref[b * width : (b + 1) * width, :], preferred_element_type=jnp.float32
        )
    rows = rows.astype(jnp.bfloat16)
    size = lead

    def place(n, carry):
        here = pl.ds(pl.multiple_of(n * size, size), size)
        names = lax.broadcasted_iota(jnp.int32, (size, vocab), 1)
        one_hot = (ids_ref[here, :] == names).astype(jnp.float32).astype(jnp.bfloat16)
        proj[here, :] = jnp.dot(one_hot, rows, preferred_element_type=jnp.float32)
        return carry

    lax.fori_loop(0, proj.shape[0] // size, place, 0)

    def convolve(n, carry):
        start = n * size + lead
        conv = [jnp.zeros((size, lanes), jnp.float32) for _ in range(3)]
        for tap in range(taps):
            here = pl.ds(pl.multiple_of(start - tap * segments, segments), size)
            piece = proj[here, :]
            for w in range(3):
                conv[w] = conv[w] + filt_ref[tap, w : w + 1, :] * piece[:, w * lanes : (w + 1) * lanes]
        there = pl.ds(pl.multiple_of(n * size, size), size)
        query[there, :] = conv[0]
        gated[there, :] = conv[1] * conv[2]
        return carry

    lax.fori_loop(0, segments * steps // size, convolve, 0)

    def spread_rows(row):
        return jnp.broadcast_to(row, (segments, lanes))

    decay = [spread_rows(jnp.exp(-rate_ref[m : m + 1, :])) for m in range(modes)]
    unroll = 4

    def ends(n, state):
        for u in range(unroll):
            row = gated[pl.ds(pl.multiple_of((n * unroll + u) * segments, segments), segments), :]
            state = tuple(d * s + row for d, s in zip(decay, state))
        return state

    zero = jnp.zeros((segments, lanes), jnp.float32)
    state = lax.fori_loop(0, steps // unroll, ends, (zero,) * modes)
    place_of = lax.broadcasted_iota(jnp.int32, (segments, lanes), 0)

    def later(value, by):
        return jnp.where(place_of >= by, pltpu.roll(value, by, 0), 0.0)

    entering = []
    for m in range(modes):
        value = later(state[m], 1)
        by = 1
        while by < segments:
            jump = jnp.exp(-rate_ref[m : m + 1, :] * float(steps * by))
            value = value + jump * later(value, by)
            by *= 2
        entering.append(value)
    strength = [
        spread_rows(residue_ref[m : m + 1, :] * jnp.sqrt(2.0 * rate_ref[m : m + 1, :]))
        for m in range(modes)
    ]
    skip = spread_rows(skip_ref[...])

    def advance(n, state):
        for u in range(unroll):
            here = pl.ds(pl.multiple_of((n * unroll + u) * segments, segments), segments)
            row = gated[here, :]
            state = tuple(d * s + row for d, s in zip(decay, state))
            terms = [c * s for c, s in zip(strength, state)]
            while len(terms) > 1:
                terms = [a + b for a, b in zip(terms[::2], terms[1::2])] + (
                    [terms[-1]] if len(terms) % 2 else []
                )
            query[here, :] = query[here, :] * (terms[0] + skip * row)
        return state

    lax.fori_loop(0, steps // unroll, advance, tuple(entering))
    for s in range(segments):
        out_ref[s] = query[pl.ds(s, steps, stride=segments), :].astype(jnp.bfloat16)


def mix(ids, gain, table, w, filt, rate, residue, skip, segments, steps):
    whole = pl.BlockSpec(memory_space=pltpu.VMEM)
    wide = w.shape[1]
    lanes = wide // 3
    return pl.pallas_call(
        mix_kernel,
        name="mix",
        out_shape=jax.ShapeDtypeStruct((segments, steps, lanes), jnp.bfloat16),
        in_specs=[whole] * 8,
        out_specs=whole,
        scratch_shapes=[
            pltpu.VMEM((ids.shape[0], wide), jnp.float32),
            pltpu.VMEM((segments * steps, lanes), jnp.float32),
            pltpu.VMEM((segments * steps, lanes), jnp.float32),
        ],
        compiler_params=pltpu.CompilerParams(vmem_limit_bytes=VMEM_BYTES),
    )(ids, gain, table, w, filt, rate, residue, skip)


def collect_kernel(
    n_ctx,
    n_dp,
    mixed_ref,
    weight_ref,
    mixed_out,
    weight_out,
    own_mixed,
    own_weight,
    a_send,
    slot_recv,
    z_send,
    w_send,
    w_recv,
    core_send,
    core_recv,
    local,
):
    me, at = lax.axis_index("ctx"), lax.axis_index("dp")
    depth, lanes = weight_ref.shape[0], mixed_ref.shape[2]
    bits = [1 << b for b in range(n_ctx.bit_length() - 1)]
    ctx_peers = [lax.rem(me + d, n_ctx) for d in range(1, n_ctx)]
    near = [(at - 1, at > 0), (at + 1, at < n_dp - 1)]
    barrier = pltpu.get_barrier_semaphore()
    dp_peers = [lax.rem(at + d, n_dp) for d in range(1, n_dp)]
    greet(ctx_peers, dp_peers)
    partner, side, up = flip(me, 1), flip(me, 2), flip(me, 4)
    across = flip(side, 4)
    half = depth // 2

    def slot(source, k):
        start = (source * n_ctx + k) * lanes
        return mixed_out.at[:, pl.ds(pl.multiple_of(start, lanes), lanes)]

    def turn(d, peer):
        return remote(mixed_ref.at[peer], slot(at, me), a_send.at[d - 1], slot_recv.at[at, me], ctx=peer)

    def block(owner, first=0, count=None):
        count = depth if count is None else count
        start = pl.multiple_of(owner * depth + first, half)
        return weight_out.at[pl.ds(start, count)]

    for d, peer in enumerate(ctx_peers):
        turn(d + 1, peer).start()
    into = [
        pltpu.make_async_copy(mixed_ref.at[me], own_mixed, local.at[0]),
        pltpu.make_async_copy(weight_ref, own_weight, local.at[1]),
    ]
    for copy in into:
        copy.start()

    def z_copy(source, d, way, hop, peer):
        k = lax.rem(me + d, n_ctx)
        src = mixed_ref.at[me] if hop == 0 and d == 0 else slot(source, k)
        return remote(src, slot(source, k), z_send.at[way, hop, d], slot_recv.at[source, k], dp=peer)

    def recv(source, d):
        k = lax.rem(me + d, n_ctx)
        z_copy_like = remote(slot(source, k), slot(source, k), z_send.at[0, 0, d], slot_recv.at[source, k], ctx=partner)
        z_copy_like.wait_recv()

    def first_hop(d):
        @pl.when(at < n_dp - 1)
        def _():
            z_copy(at, d, 0, 0, at + 1).start()

        @pl.when(at > 0)
        def _():
            z_copy(at, d, 1, 0, at - 1).start()

    first_hop(0)
    own = [
        remote(weight_ref, block(me), w_send.at[0], w_recv.at[0], ctx=side),
        remote(weight_ref, block(me), w_send.at[1], w_recv.at[1], ctx=up),
        remote(weight_ref, block(me), w_send.at[2], w_recv.at[2], ctx=partner),
    ]
    for copy in own:
        copy.start()
    for copy in into:
        copy.wait()
    out = [
        pltpu.make_async_copy(own_mixed, slot(at, me), local.at[0]),
        pltpu.make_async_copy(own_weight, block(me), local.at[1]),
    ]
    for copy in out:
        copy.start()
    for d in range(1, n_ctx):
        recv(at, d)
        first_hop(d)

    for hop in range(1, n_dp):
        for d in range(n_ctx):

            @pl.when(at - hop >= 0)
            def _():
                recv(at - hop, d)

                if hop < n_dp - 1:

                    @pl.when(at < n_dp - 1)
                    def _():
                        z_copy(at - hop, d, 0, hop, at + 1).start()

            @pl.when(at + hop <= n_dp - 1)
            def _():
                recv(at + hop, d)

                if hop < n_dp - 1:

                    @pl.when(at > 0)
                    def _():
                        z_copy(at + hop, d, 1, hop, at - 1).start()

        if hop == 1:
            own[0].wait_recv()
            own[1].wait_recv()
            passed = [
                remote(block(side, 0, half), block(side, 0, half), w_send.at[3], w_recv.at[3], ctx=up),
                remote(block(up, half, half), block(up, half, half), w_send.at[4], w_recv.at[4], ctx=side),
                remote(block(side), block(side), core_send.at[0], core_recv.at[0], ctx=partner),
                remote(block(up), block(up), core_send.at[1], core_recv.at[1], ctx=partner),
            ]
            for copy in passed:
                copy.start()
    passed[0].wait_recv()
    passed[1].wait_recv()
    last = [
        remote(block(across, 0, half), block(across, 0, half), core_send.at[2], core_recv.at[2], ctx=partner),
        remote(block(across, half, half), block(across, half, half), core_send.at[3], core_recv.at[3], ctx=partner),
    ]
    for copy in last:
        copy.start()
    own[2].wait_recv()
    passed[2].wait_recv()
    passed[3].wait_recv()
    for copy in last:
        copy.wait_recv()
    for copy in own + passed + last:
        copy.wait_send()
    for d, peer in enumerate(ctx_peers):
        turn(d + 1, peer).wait_send()
    for hop in range(n_dp - 1):
        for d in range(n_ctx):

            @pl.when((at - hop >= 0) & (at < n_dp - 1))
            def _():
                z_copy(at - hop, d, 0, hop, at + 1).wait_send()

            @pl.when((at + hop <= n_dp - 1) & (at > 0))
            def _():
                z_copy(at + hop, d, 1, hop, at - 1).wait_send()

    for copy in out:
        copy.wait()


def collect(n_ctx, n_dp, mixed, weight):
    depth, columns = weight.shape
    steps, lanes = mixed.shape[1:]
    anywhere = pl.BlockSpec(memory_space=pl.ANY)
    dma = pltpu.SemaphoreType.DMA
    return pl.pallas_call(
        lambda *refs: collect_kernel(n_ctx, n_dp, *refs),
        name="collect",
        out_shape=(
            jax.ShapeDtypeStruct((steps, n_dp * n_ctx * lanes), mixed.dtype),
            jax.ShapeDtypeStruct((n_ctx * depth, columns), weight.dtype),
        ),
        in_specs=[anywhere] * 2,
        out_specs=[anywhere] * 2,
        scratch_shapes=[
            pltpu.VMEM((steps, lanes), mixed.dtype),
            pltpu.VMEM((depth, columns), weight.dtype),
            dma((n_ctx - 1,)),
            dma((n_dp, n_ctx)),
            dma((2, n_dp - 1, n_ctx)),
            dma((5,)),
            dma((5,)),
            dma((4,)),
            dma((4,)),
            dma((2,)),
        ],
        compiler_params=pltpu.CompilerParams(
            collective_id=1, has_side_effects=True, vmem_limit_bytes=8 << 20
        ),
    )(mixed, weight)


def by_channel(
    n_ctx,
    n_dp,
    ids,
    embed_table,
    norm_gain,
    w_query,
    w_key,
    w_value,
    short_filter,
    pole_rate,
    residue,
    skip_gain,
    w_out,
):
    vocab = embed_table.shape[0]
    tok_rows = ids.shape[0]
    taps = short_filter.shape[0]
    me = lax.axis_index("ctx")
    gain = norm_gain.astype(jnp.float32).reshape(-1, LANES)
    all_ids, all_gain, all_table, w_mine = spread(
        n_ctx, n_dp, ids.reshape(-1, LANES), gain, embed_table, w_query, w_key, w_value
    )
    all_gain = all_gain.reshape(1, -1)
    by_step = all_ids.reshape(n_ctx, tok_rows)
    before = jnp.concatenate(
        [jnp.full((1, taps - 1), -1, jnp.int32), by_step[:-1, tok_rows - (taps - 1) :]], axis=0
    )
    pad = jnp.full((LANES - n_ctx * (taps - 1),), -1, jnp.int32)
    ordered = jnp.concatenate([pad, before.T.reshape(-1), by_step.T.reshape(-1)])[:, None]

    def mine(value, axis):
        return lax.dynamic_slice_in_dim(value, me * LANES, LANES, axis)

    mixed = mix(
        ordered,
        all_gain,
        all_table,
        w_mine,
        mine(short_filter, 2),
        mine(pole_rate, 0).T,
        mine(residue, 0).T,
        mine(skip_gain, 0)[None, :],
        n_ctx,
        tok_rows,
    )
    all_mixed, all_rows = collect(n_ctx, n_dp, mixed, w_out)
    one_hot = (ids[:, None] == jnp.arange(vocab, dtype=jnp.int32)[None, :]).astype(jnp.bfloat16)
    embedded = jnp.dot(one_hot, embed_table, preferred_element_type=jnp.float32)
    output = jnp.dot(all_mixed, all_rows, preferred_element_type=jnp.float32)
    return (embedded + output).astype(jnp.bfloat16)


def solution(mesh):
    placed = (
        P("ctx"),
        P(None, "dp"),
        P("dp"),
        P("ctx", "dp"),
        P("ctx", "dp"),
        P("ctx", "dp"),
        P(None, None, "dp"),
        P("dp", None),
        P("dp", None),
        P("dp"),
        P("ctx", "dp"),
    )
    n_ctx, n_dp = mesh.shape["ctx"], mesh.shape["dp"]

    def body(*args):
        ids, w_query = args[0], args[3]
        fits = (
            n_ctx == SUBLANES
            and n_dp > 1
            and w_query.shape[1] == n_ctx * LANES
            and ids.shape[0] % LANES == 0
        )
        if fits:
            return by_channel(n_ctx, n_dp, *args)
        return shards(*args)

    return jax.shard_map(
        body, mesh=mesh, in_specs=placed, out_specs=P("ctx", "dp"), check_vma=False
    )
```

```python
import math

import jax
import jax.numpy as jnp
from jax import lax

from jax.experimental import pallas as pl
from jax.experimental.pallas import tpu as pltpu
from jax.sharding import PartitionSpec as P

MESH = pl.DeviceIdType.MESH
LANES = 128
SUBLANES = 8
VMEM_BYTES = 36 << 20


def shifted(value, axis, steps):
    count = lax.axis_size(axis)
    initial, last = (max(0, -steps), min(count, count - steps))
    return lax.ppermute(value, axis, [(source, source + steps) for source in range(initial, last)])


def entering_2(value, axis, combine, identity):
    peers, index = (lax.axis_size(axis), lax.axis_index(axis))
    everything = jax.tree.map(lambda part: lax.all_gather(part, axis), value)
    start = jax.tree.map(
        lambda part, zero: jnp.broadcast_to(jnp.asarray(zero, part.dtype), part.shape),
        value,
        identity,
    )

    def turn(k, before):
        reached = k < index
        new = combine(before, jax.tree.map(lambda part: part[k], everything))
        return jax.tree.map(lambda a, b: jnp.where(reached, a, b), new, before)

    return lax.fori_loop(0, peers, turn, start)


def shards(
    ids,
    embed_table,
    norm_gain,
    w_query,
    w_key,
    w_value,
    short_filter,
    pole_rate,
    residue,
    skip_gain,
    w_out,
):
    highest = lax.Precision.HIGHEST
    vocab = embed_table.shape[0]
    channels = w_query.shape[1]
    one_hot = (ids[:, None] == jnp.arange(vocab, dtype=jnp.int32)[None, :]).astype(jnp.bfloat16)
    embedded = jnp.dot(one_hot, embed_table, preferred_element_type=jnp.float32).astype(
        jnp.bfloat16
    )
    full_rows, full_gain = (
        lax.all_gather(embedded, "dp", axis=1, tiled=True),
        lax.all_gather(norm_gain, "dp", axis=0, tiled=True),
    )
    floated = full_rows.astype(jnp.float32)
    scale = lax.rsqrt(jnp.mean(floated * floated, axis=1, keepdims=True) + 1e-06)
    normed = (floated * scale * full_gain.astype(jnp.float32)[None, :]).astype(jnp.bfloat16)
    tok_rows = normed.shape[0]

    def add_rows(piece):
        return jnp.dot(normed, piece, preferred_element_type=jnp.float32)

    query_proj = add_rows(lax.all_gather(w_query, "ctx", axis=0, tiled=True))
    key_proj = add_rows(lax.all_gather(w_key, "ctx", axis=0, tiled=True))
    value_proj = add_rows(lax.all_gather(w_value, "ctx", axis=0, tiled=True))
    projected = jnp.concatenate([query_proj, key_proj, value_proj], axis=1).astype(jnp.bfloat16)
    taps = short_filter.shape[0]
    previous = shifted(projected[tok_rows - (taps - 1) :], "ctx", 1)
    extended = jnp.concatenate([previous, projected], axis=0).astype(jnp.float32)
    filt_rows = short_filter.reshape(taps, 3 * channels)
    convolved = jnp.zeros((tok_rows, 3 * channels), jnp.float32)
    for tap in range(taps):
        convolved = (
            convolved
            + filt_rows[tap][None, :] * extended[taps - 1 - tap : taps - 1 - tap + tok_rows]
        )
    query_conv = convolved[:, :channels]
    gated = convolved[:, channels : 2 * channels] * convolved[:, 2 * channels :]
    sub_len = math.gcd(tok_rows, 64)
    blocks = tok_rows // sub_len
    lag_index = jnp.arange(sub_len, dtype=jnp.int32)
    lags = lag_index.astype(jnp.float32)
    strength = residue * jnp.sqrt(2.0 * pole_rate)
    kernel = jnp.einsum(
        "lck,ck->lc", jnp.exp(-pole_rate[None] * lags[:, None, None]), strength, precision=highest
    )
    offsets = lag_index[:, None] - lag_index[None, :]
    toeplitz = jnp.where((offsets >= 0)[:, :, None], kernel[jnp.maximum(offsets, 0)], 0.0)
    pieces = gated.reshape(blocks, sub_len, channels)
    inside = jnp.einsum("tsc,bsc->btc", toeplitz, pieces, precision=highest)
    tail_decay = jnp.exp(-pole_rate[None] * (sub_len - 1.0 - lags)[:, None, None])
    block_ends = jnp.einsum("sck,bsc->bck", tail_decay, pieces, precision=highest)
    step_decay = jnp.exp(-pole_rate * float(sub_len))

    def advance(state, block_end):
        return (step_decay * state + block_end, state)

    device_end, entering = lax.scan(advance, jnp.zeros_like(step_decay), block_ends)
    device_decay = jnp.exp(-pole_rate * float(tok_rows))

    def combine(earlier, later):
        return (earlier[0] * later[0], later[0] * earlier[1] + later[1])

    decay_total, incoming = entering_2(
        (device_decay, device_end),
        "ctx",
        combine,
        (jnp.ones_like(device_decay), jnp.zeros_like(device_end)),
    )
    block_pos = jnp.arange(blocks, dtype=jnp.float32) * float(sub_len)
    states_in = entering + jnp.exp(-pole_rate[None] * block_pos[:, None, None]) * incoming[None]
    lead = jnp.exp(-pole_rate[None] * (lags + 1.0)[:, None, None]) * strength[None]
    carried = jnp.einsum("tck,bck->btc", lead, states_in, precision=highest)
    long_conv = (inside + carried).reshape(tok_rows, channels) + skip_gain[None, :] * gated
    mixed = (query_conv * long_conv).astype(jnp.bfloat16)
    all_mixed = lax.all_gather(mixed, "dp", axis=1, tiled=True)
    output = jnp.dot(
        all_mixed,
        lax.all_gather(w_out, "ctx", axis=0, tiled=True),
        preferred_element_type=jnp.float32,
    )
    return (embedded.astype(jnp.float32) + output).astype(jnp.bfloat16)


def remote(src, dst, send, recv, **where):
    return pltpu.make_async_remote_copy(
        src_ref=src,
        dst_ref=dst,
        send_sem=send,
        recv_sem=recv,
        device_id=where,
        device_id_type=MESH,
    )


def greet(ctx_peers, dp_peers):
    barrier = pltpu.get_barrier_semaphore()
    for peer in ctx_peers:
        pl.semaphore_signal(barrier, inc=1, device_id={"ctx": peer}, device_id_type=MESH)
    for peer in dp_peers:
        pl.semaphore_signal(barrier, inc=1, device_id={"dp": peer}, device_id_type=MESH)
    pl.semaphore_wait(barrier, len(ctx_peers) + len(dp_peers))


def flip(index, bit):
    return index + bit - 2 * bit * (lax.rem(index // bit, 2))


def spread_kernel(
    n_ctx,
    n_dp,
    ids_ref,
    gain_ref,
    table_ref,
    wq_ref,
    wk_ref,
    wv_ref,
    ids_out,
    gain_out,
    table_out,
    w_out,
    own_w,
    own_table,
    w_send,
    w_recv,
    id_send,
    id_recv,
    gain_send,
    gain_recv,
    z_send,
    z_recv,
    core_send,
    core_recv,
    local,
):
    me, at = lax.axis_index("ctx"), lax.axis_index("dp")
    depth, wide = wq_ref.shape[0], wq_ref.shape[1] // n_ctx
    vocab = table_ref.shape[0]
    chunks = z_send.shape[2]
    part = vocab // 2 // chunks
    partner = flip(me, 1)
    ctx_peers = [lax.rem(me + d, n_ctx) for d in range(1, n_ctx)]
    dp_peers = [lax.rem(at + d, n_dp) for d in range(1, n_dp)]
    greet(ctx_peers, dp_peers)
    rows = pl.ds(pl.multiple_of(me * depth, depth), depth)
    weights = (wq_ref, wk_ref, wv_ref)

    def half_chunk(core, k):
        return pl.ds(pl.multiple_of((core * chunks + k) * part, part), part)

    def z_copy(source, k, way, hop, peer):
        piece = half_chunk(lax.rem(me, 2), k)
        src = table_ref.at[piece] if hop == 0 else table_out.at[source, piece]
        return remote(
            src,
            table_out.at[source, piece],
            z_send.at[way, hop, k],
            z_recv.at[source, k],
            dp=peer,
        )

    def core_copy(source, core, k):
        piece = half_chunk(core, k)
        return remote(
            table_out.at[source, piece],
            table_out.at[source, piece],
            core_send.at[source, k],
            core_recv.at[source, k],
            ctx=partner,
        )

    for k in range(chunks):

        @pl.when(at < n_dp - 1)
        def _():
            z_copy(at, k, 0, 0, at + 1).start()

        @pl.when(at > 0)
        def _():
            z_copy(at, k, 1, 0, at - 1).start()

    sends = []
    for d, peer in enumerate(ctx_peers):
        copy = remote(ids_ref, ids_out.at[me], id_send.at[d], id_recv.at[me], ctx=peer)
        copy.start()
        sends.append(copy)
    for d, peer in enumerate(dp_peers):
        copy = remote(gain_ref, gain_out.at[at], gain_send.at[d], gain_recv.at[at], dp=peer)
        copy.start()
        sends.append(copy)
    for d, peer in enumerate(ctx_peers):
        for w, weight in enumerate(weights):
            copy = remote(
                weight.at[:, pl.ds(pl.multiple_of(peer * wide, wide), wide)],
                w_out.at[rows, pl.ds(w * wide, wide)],
                w_send.at[d, w],
                w_recv.at[me, w],
                ctx=peer,
            )
            copy.start()
            sends.append(copy)
    into = [
        pltpu.make_async_copy(
            weight.at[:, pl.ds(pl.multiple_of(me * wide, wide), wide)],
            own_w.at[:, pl.ds(w * wide, wide)],
            local.at[w],
        )
        for w, weight in enumerate(weights)
    ]
    into.append(pltpu.make_async_copy(table_ref, own_table, local.at[3]))
    into.append(pltpu.make_async_copy(ids_ref, ids_out.at[me], local.at[4]))
    into.append(pltpu.make_async_copy(gain_ref, gain_out.at[at], local.at[5]))
    for copy in into:
        copy.start()
    for copy in into:
        copy.wait()
    out = [
        pltpu.make_async_copy(own_w, w_out.at[rows], local.at[0]),
        pltpu.make_async_copy(own_table, table_out.at[at], local.at[1]),
    ]
    for copy in out:
        copy.start()

    core = lax.rem(me, 2)
    for hop in range(1, n_dp):
        for k in range(chunks):

            @pl.when(at - hop >= 0)
            def _():
                z_copy(at - hop, k, 0, 0, at).wait_recv()
                core_copy(at - hop, core, k).start()

                if hop < n_dp - 1:

                    @pl.when(at < n_dp - 1)
                    def _():
                        z_copy(at - hop, k, 0, hop, at + 1).start()

            @pl.when(at + hop <= n_dp - 1)
            def _():
                z_copy(at + hop, k, 1, 0, at).wait_recv()
                core_copy(at + hop, core, k).start()

                if hop < n_dp - 1:

                    @pl.when(at > 0)
                    def _():
                        z_copy(at + hop, k, 1, hop, at - 1).start()

    for d in range(1, n_dp):
        source = lax.rem(at + d, n_dp)
        for k in range(chunks):
            core_copy(source, 1 - core, k).wait_recv()
            core_copy(source, core, k).wait_send()
    for hop in range(n_dp - 1):
        for k in range(chunks):

            @pl.when((at - hop >= 0) & (at < n_dp - 1))
            def _():
                z_copy(at - hop, k, 0, hop, at + 1).wait_send()

            @pl.when((at + hop <= n_dp - 1) & (at > 0))
            def _():
                z_copy(at + hop, k, 1, hop, at - 1).wait_send()

    for d, peer in enumerate(ctx_peers):
        remote(ids_ref, ids_out.at[peer], id_send.at[d], id_recv.at[peer], ctx=peer).wait_recv()
        theirs = pl.ds(pl.multiple_of(peer * depth, depth), depth)
        for w, weight in enumerate(weights):
            remote(
                weight.at[:, pl.ds(pl.multiple_of(peer * wide, wide), wide)],
                w_out.at[theirs, pl.ds(w * wide, wide)],
                w_send.at[d, w],
                w_recv.at[peer, w],
                ctx=peer,
            ).wait_recv()
    for d, peer in enumerate(dp_peers):
        remote(gain_ref, gain_out.at[peer], gain_send.at[d], gain_recv.at[peer], dp=peer).wait_recv()
    for copy in sends:
        copy.wait_send()
    for copy in out:
        copy.wait()


def spread(n_ctx, n_dp, ids, gain, table, w_query, w_key, w_value):
    depth, wide = w_query.shape[0], w_query.shape[1] // n_ctx
    chunks = 2
    anywhere = pl.BlockSpec(memory_space=pl.ANY)
    dma = pltpu.SemaphoreType.DMA
    return pl.pallas_call(
        lambda *refs: spread_kernel(n_ctx, n_dp, *refs),
        name="spread",
        out_shape=(
            jax.ShapeDtypeStruct((n_ctx, *ids.shape), ids.dtype),
            jax.ShapeDtypeStruct((n_dp, *gain.shape), gain.dtype),
            jax.ShapeDtypeStruct((n_dp, *table.shape), table.dtype),
            jax.ShapeDtypeStruct((n_ctx * depth, 3 * wide), w_query.dtype),
        ),
        in_specs=[anywhere] * 6,
        out_specs=[anywhere] * 4,
        scratch_shapes=[
            pltpu.VMEM((depth, 3 * wide), w_query.dtype),
            pltpu.VMEM(table.shape, table.dtype),
            dma((n_ctx - 1, 3)),
            dma((n_ctx, 3)),
            dma((n_ctx - 1,)),
            dma((n_ctx,)),
            dma((n_dp - 1,)),
            dma((n_dp,)),
            dma((2, n_dp - 1, chunks)),
            dma((n_dp, chunks)),
            dma((n_dp, chunks)),
            dma((n_dp, chunks)),
            dma((6,)),
        ],
        compiler_params=pltpu.CompilerParams(
            collective_id=0, has_side_effects=True, vmem_limit_bytes=56 << 20
        ),
    )(ids, gain, table, w_query, w_key, w_value)


def mix_kernel(
    me_ref,
    ids_ref,
    gain_ref,
    table_ref,
    w_ref,
    filt_ref,
    rate_ref,
    residue_ref,
    skip_ref,
    out_ref,
    proj,
    gated,
    query,
):
    n_dp, vocab, width = table_ref.shape
    features = n_dp * width
    taps = filt_ref.shape[0]
    modes = rate_ref.shape[1]
    segments, steps, lanes = out_ref.shape
    lead = proj.shape[1] - segments * steps
    mine = pl.ds(pl.multiple_of(me_ref[0] * lanes, lanes), lanes)
    total = jnp.zeros((vocab, 1), jnp.float32)
    for b in range(n_dp):
        block = table_ref[b].astype(jnp.float32)
        total = total + jnp.sum(block * block, axis=1, keepdims=True)
    scale = lax.rsqrt(total / features + 1e-06)
    rows = jnp.zeros((vocab, 3 * lanes), jnp.float32)
    for b in range(n_dp):
        block = table_ref[b].astype(jnp.float32)
        gain = jnp.concatenate([gain_ref[b, r : r + 1, :] for r in range(width // lanes)], axis=1)
        normed = (block * scale * gain).astype(jnp.bfloat16)
        rows = rows + jnp.dot(
            normed, w_ref[b * width : (b + 1) * width, :], preferred_element_type=jnp.float32
        )
    rows = rows.astype(jnp.bfloat16)
    pieces = steps // lanes
    per_segment = ids_ref.shape[1]
    names = lax.broadcasted_iota(jnp.int32, (lanes, vocab), 1)
    for s in range(segments):
        by_lane = ids_ref[s].astype(jnp.float32)
        square = jnp.concatenate(
            [by_lane, jnp.zeros((lanes - per_segment, lanes), jnp.float32)], axis=0
        )
        columns = square.T.astype(jnp.int32)
        one_hot = jnp.concatenate(
            [
                (columns[:, p : p + 1] == names).astype(jnp.float32).astype(jnp.bfloat16)
                for p in range(pieces)
            ],
            axis=0,
        )
        picked = jnp.dot(one_hot, rows, preferred_element_type=jnp.float32)
        for w in range(3):
            proj[w, pl.ds(lead + s, steps, stride=segments), :] = picked[:, w * lanes : (w + 1) * lanes]
    place_of = lax.broadcasted_iota(jnp.int32, (segments, lanes), 0)

    def later(value, by):
        return jnp.where(place_of >= by, pltpu.roll(value, by, 0), 0.0)

    end = proj.shape[1]
    for tap in range(1, taps):
        for w in range(3):
            tail = proj[w, end - tap * segments : end - (tap - 1) * segments, :]
            proj[w, lead - tap * segments : lead - (tap - 1) * segments, :] = later(tail, 1)
    size = lanes

    def convolve(n, carry):
        start = n * size + lead
        conv = [jnp.zeros((size, lanes), jnp.float32) for _ in range(3)]
        for tap in range(taps):
            here = pl.ds(pl.multiple_of(start - tap * segments, segments), size)
            for w in range(3):
                conv[w] = conv[w] + filt_ref[tap, w : w + 1, mine] * proj[w, here, :]
        there = pl.ds(pl.multiple_of(n * size, size), size)
        query[there, :] = conv[0]
        gated[there, :] = conv[1] * conv[2]
        return carry

    lax.fori_loop(0, segments * steps // size, convolve, 0)

    def spread_rows(row):
        return jnp.broadcast_to(row, (segments, lanes))

    def turned(ref):
        value = ref[mine, :]
        return jnp.concatenate([value, jnp.zeros((lanes, lanes - modes), jnp.float32)], axis=1).T

    rate, residue = turned(rate_ref), turned(residue_ref)
    decay = [spread_rows(jnp.exp(-rate[m : m + 1, :])) for m in range(modes)]
    unroll = 4

    def ends(n, state):
        for u in range(unroll):
            row = gated[pl.ds(pl.multiple_of((n * unroll + u) * segments, segments), segments), :]
            state = tuple(d * s + row for d, s in zip(decay, state))
        return state

    zero = jnp.zeros((segments, lanes), jnp.float32)
    state = lax.fori_loop(0, steps // unroll, ends, (zero,) * modes)
    entering = []
    for m in range(modes):
        value = later(state[m], 1)
        by = 1
        while by < segments:
            jump = jnp.exp(-rate[m : m + 1, :] * float(steps * by))
            value = value + jump * later(value, by)
            by *= 2
        entering.append(value)
    strength = [
        spread_rows(residue[m : m + 1, :] * jnp.sqrt(2.0 * rate[m : m + 1, :])) for m in range(modes)
    ]
    skip = spread_rows(skip_ref[:, mine])

    def advance(n, state):
        for u in range(unroll):
            here = pl.ds(pl.multiple_of((n * unroll + u) * segments, segments), segments)
            row = gated[here, :]
            sums = [skip * row, None]
            new = []
            for m in range(modes):
                now = decay[m] * state[m] + row
                new.append(now)
                term = strength[m] * now
                sums[m % 2] = term if sums[m % 2] is None else sums[m % 2] + term
            state = tuple(new)
            query[here, :] = query[here, :] * (sums[0] + sums[1])
        return state

    lax.fori_loop(0, steps // unroll, advance, tuple(entering))
    for s in range(segments):
        out_ref[s] = query[pl.ds(s, steps, stride=segments), :].astype(jnp.bfloat16)


def mix(me, ids, gain, table, w, filt, rate, residue, skip, segments, steps):
    whole = pl.BlockSpec(memory_space=pltpu.VMEM)
    lanes = w.shape[1] // 3
    lead = segments * (filt.shape[0] - 1)
    return pl.pallas_call(
        mix_kernel,
        name="mix",
        out_shape=jax.ShapeDtypeStruct((segments, steps, lanes), jnp.bfloat16),
        in_specs=[pl.BlockSpec(memory_space=pltpu.SMEM)] + [whole] * 8,
        out_specs=whole,
        scratch_shapes=[
            pltpu.VMEM((3, lead + segments * steps, lanes), jnp.float32),
            pltpu.VMEM((segments * steps, lanes), jnp.float32),
            pltpu.VMEM((segments * steps, lanes), jnp.float32),
        ],
        compiler_params=pltpu.CompilerParams(vmem_limit_bytes=VMEM_BYTES),
    )(me, ids, gain, table, w, filt, rate, residue, skip)


def collect_kernel(
    n_ctx,
    n_dp,
    mixed_ref,
    weight_ref,
    mixed_out,
    weight_out,
    own_mixed,
    own_weight,
    a_send,
    slot_recv,
    z_send,
    w_send,
    w_recv,
    core_send,
    core_recv,
    local,
):
    me, at = lax.axis_index("ctx"), lax.axis_index("dp")
    depth, lanes = weight_ref.shape[0], mixed_ref.shape[2]
    bits = [1 << b for b in range(n_ctx.bit_length() - 1)]
    ctx_peers = [lax.rem(me + d, n_ctx) for d in range(1, n_ctx)]
    near = [(at - 1, at > 0), (at + 1, at < n_dp - 1)]
    barrier = pltpu.get_barrier_semaphore()
    dp_peers = [lax.rem(at + d, n_dp) for d in range(1, n_dp)]
    greet(ctx_peers, dp_peers)
    partner, side, up = flip(me, 1), flip(me, 2), flip(me, 4)
    across = flip(side, 4)
    half = depth // 2

    def slot(source, k):
        start = (source * n_ctx + k) * lanes
        return mixed_out.at[:, pl.ds(pl.multiple_of(start, lanes), lanes)]

    def turn(d, peer):
        return remote(mixed_ref.at[peer], slot(at, me), a_send.at[d - 1], slot_recv.at[at, me], ctx=peer)

    def block(owner, first=0, count=None):
        count = depth if count is None else count
        start = pl.multiple_of(owner * depth + first, half)
        return weight_out.at[pl.ds(start, count)]

    for d, peer in enumerate(ctx_peers):
        turn(d + 1, peer).start()
    into = [
        pltpu.make_async_copy(mixed_ref.at[me], own_mixed, local.at[0]),
        pltpu.make_async_copy(weight_ref, own_weight, local.at[1]),
    ]
    for copy in into:
        copy.start()

    def z_copy(source, d, way, hop, peer):
        k = lax.rem(me + d, n_ctx)
        src = mixed_ref.at[me] if hop == 0 and d == 0 else slot(source, k)
        return remote(src, slot(source, k), z_send.at[way, hop, d], slot_recv.at[source, k], dp=peer)

    def recv(source, d):
        k = lax.rem(me + d, n_ctx)
        z_copy_like = remote(slot(source, k), slot(source, k), z_send.at[0, 0, d], slot_recv.at[source, k], ctx=partner)
        z_copy_like.wait_recv()

    def first_hop(d):
        @pl.when(at < n_dp - 1)
        def _():
            z_copy(at, d, 0, 0, at + 1).start()

        @pl.when(at > 0)
        def _():
            z_copy(at, d, 1, 0, at - 1).start()

    first_hop(0)
    own = [
        remote(weight_ref, block(me), w_send.at[0], w_recv.at[0], ctx=side),
        remote(weight_ref, block(me), w_send.at[1], w_recv.at[1], ctx=up),
        remote(weight_ref, block(me), w_send.at[2], w_recv.at[2], ctx=partner),
    ]
    own[2].start()
    for copy in into:
        copy.wait()
    out = [
        pltpu.make_async_copy(own_mixed, slot(at, me), local.at[0]),
        pltpu.make_async_copy(own_weight, block(me), local.at[1]),
    ]
    for copy in out:
        copy.start()
    for d in range(1, n_ctx):
        recv(at, d)
        first_hop(d)
    own[0].start()
    own[1].start()

    for hop in range(1, n_dp):
        for d in range(n_ctx):

            @pl.when(at - hop >= 0)
            def _():
                recv(at - hop, d)

                if hop < n_dp - 1:

                    @pl.when(at < n_dp - 1)
                    def _():
                        z_copy(at - hop, d, 0, hop, at + 1).start()

            @pl.when(at + hop <= n_dp - 1)
            def _():
                recv(at + hop, d)

                if hop < n_dp - 1:

                    @pl.when(at > 0)
                    def _():
                        z_copy(at + hop, d, 1, hop, at - 1).start()

        if hop == 1:
            own[0].wait_recv()
            own[1].wait_recv()
            passed = [
                remote(block(side, 0, half), block(side, 0, half), w_send.at[3], w_recv.at[3], ctx=up),
                remote(block(up, half, half), block(up, half, half), w_send.at[4], w_recv.at[4], ctx=side),
                remote(block(side), block(side), core_send.at[0], core_recv.at[0], ctx=partner),
                remote(block(up), block(up), core_send.at[1], core_recv.at[1], ctx=partner),
            ]
            for copy in passed:
                copy.start()
    passed[0].wait_recv()
    passed[1].wait_recv()
    last = [
        remote(block(across, 0, half), block(across, 0, half), core_send.at[2], core_recv.at[2], ctx=partner),
        remote(block(across, half, half), block(across, half, half), core_send.at[3], core_recv.at[3], ctx=partner),
    ]
    for copy in last:
        copy.start()
    own[2].wait_recv()
    passed[2].wait_recv()
    passed[3].wait_recv()
    for copy in last:
        copy.wait_recv()
    for copy in own + passed + last:
        copy.wait_send()
    for d, peer in enumerate(ctx_peers):
        turn(d + 1, peer).wait_send()
    for hop in range(n_dp - 1):
        for d in range(n_ctx):

            @pl.when((at - hop >= 0) & (at < n_dp - 1))
            def _():
                z_copy(at - hop, d, 0, hop, at + 1).wait_send()

            @pl.when((at + hop <= n_dp - 1) & (at > 0))
            def _():
                z_copy(at + hop, d, 1, hop, at - 1).wait_send()

    for copy in out:
        copy.wait()


def collect(n_ctx, n_dp, mixed, weight):
    depth, columns = weight.shape
    steps, lanes = mixed.shape[1:]
    anywhere = pl.BlockSpec(memory_space=pl.ANY)
    dma = pltpu.SemaphoreType.DMA
    return pl.pallas_call(
        lambda *refs: collect_kernel(n_ctx, n_dp, *refs),
        name="collect",
        out_shape=(
            jax.ShapeDtypeStruct((steps, n_dp * n_ctx * lanes), mixed.dtype),
            jax.ShapeDtypeStruct((n_ctx * depth, columns), weight.dtype),
        ),
        in_specs=[anywhere] * 2,
        out_specs=[anywhere] * 2,
        scratch_shapes=[
            pltpu.VMEM((steps, lanes), mixed.dtype),
            pltpu.VMEM((depth, columns), weight.dtype),
            dma((n_ctx - 1,)),
            dma((n_dp, n_ctx)),
            dma((2, n_dp - 1, n_ctx)),
            dma((5,)),
            dma((5,)),
            dma((4,)),
            dma((4,)),
            dma((2,)),
        ],
        compiler_params=pltpu.CompilerParams(
            collective_id=1, has_side_effects=True, vmem_limit_bytes=8 << 20
        ),
    )(mixed, weight)


def by_channel(
    n_ctx,
    n_dp,
    ids,
    embed_table,
    norm_gain,
    w_query,
    w_key,
    w_value,
    short_filter,
    pole_rate,
    residue,
    skip_gain,
    w_out,
):
    vocab = embed_table.shape[0]
    tok_rows = ids.shape[0]
    gain = norm_gain.astype(jnp.float32).reshape(-1, LANES)
    by_lane = ids.reshape(-1, LANES)
    by_lane = jnp.pad(by_lane, ((0, -by_lane.shape[0] % SUBLANES), (0, 0)))
    all_ids, all_gain, all_table, w_mine = spread(
        n_ctx, n_dp, by_lane, gain, embed_table, w_query, w_key, w_value
    )
    mixed = mix(
        lax.axis_index("ctx").astype(jnp.int32).reshape(1),
        all_ids,
        all_gain,
        all_table,
        w_mine,
        short_filter,
        pole_rate,
        residue,
        skip_gain[None, :],
        n_ctx,
        tok_rows,
    )
    all_mixed, all_rows = collect(n_ctx, n_dp, mixed, w_out)
    one_hot = (ids[:, None] == jnp.arange(vocab, dtype=jnp.int32)[None, :]).astype(jnp.bfloat16)
    embedded = jnp.dot(one_hot, embed_table, preferred_element_type=jnp.float32)
    output = jnp.dot(all_mixed, all_rows, preferred_element_type=jnp.float32)
    return (embedded + output).astype(jnp.bfloat16)


def solution(mesh):
    placed = (
        P("ctx"),
        P(None, "dp"),
        P("dp"),
        P("ctx", "dp"),
        P("ctx", "dp"),
        P("ctx", "dp"),
        P(None, None, "dp"),
        P("dp", None),
        P("dp", None),
        P("dp"),
        P("ctx", "dp"),
    )
    n_ctx, n_dp = mesh.shape["ctx"], mesh.shape["dp"]

    def body(*args):
        ids, w_query = args[0], args[3]
        fits = (
            n_ctx == SUBLANES
            and n_dp > 1
            and w_query.shape[1] == n_ctx * LANES
            and ids.shape[0] % LANES == 0
        )
        if fits:
            return by_channel(n_ctx, n_dp, *args)
        return shards(*args)

    return jax.shard_map(
        body, mesh=mesh, in_specs=placed, out_specs=P("ctx", "dp"), check_vma=False
    )
```

```python
import math

import jax
import jax.numpy as jnp
from jax import lax

from jax.experimental import pallas as pl
from jax.experimental.pallas import tpu as pltpu
from jax.sharding import PartitionSpec as P

MESH = pl.DeviceIdType.MESH
LANES = 128
SUBLANES = 8
VMEM_BYTES = 36 << 20


def shifted(value, axis, steps):
    count = lax.axis_size(axis)
    initial, last = (max(0, -steps), min(count, count - steps))
    return lax.ppermute(value, axis, [(source, source + steps) for source in range(initial, last)])


def entering_2(value, axis, combine, identity):
    peers, index = (lax.axis_size(axis), lax.axis_index(axis))
    everything = jax.tree.map(lambda part: lax.all_gather(part, axis), value)
    start = jax.tree.map(
        lambda part, zero: jnp.broadcast_to(jnp.asarray(zero, part.dtype), part.shape),
        value,
        identity,
    )

    def turn(k, before):
        reached = k < index
        new = combine(before, jax.tree.map(lambda part: part[k], everything))
        return jax.tree.map(lambda a, b: jnp.where(reached, a, b), new, before)

    return lax.fori_loop(0, peers, turn, start)


def shards(
    ids,
    embed_table,
    norm_gain,
    w_query,
    w_key,
    w_value,
    short_filter,
    pole_rate,
    residue,
    skip_gain,
    w_out,
):
    highest = lax.Precision.HIGHEST
    vocab = embed_table.shape[0]
    channels = w_query.shape[1]
    one_hot = (ids[:, None] == jnp.arange(vocab, dtype=jnp.int32)[None, :]).astype(jnp.bfloat16)
    embedded = jnp.dot(one_hot, embed_table, preferred_element_type=jnp.float32).astype(
        jnp.bfloat16
    )
    full_rows, full_gain = (
        lax.all_gather(embedded, "dp", axis=1, tiled=True),
        lax.all_gather(norm_gain, "dp", axis=0, tiled=True),
    )
    floated = full_rows.astype(jnp.float32)
    scale = lax.rsqrt(jnp.mean(floated * floated, axis=1, keepdims=True) + 1e-06)
    normed = (floated * scale * full_gain.astype(jnp.float32)[None, :]).astype(jnp.bfloat16)
    tok_rows = normed.shape[0]

    def add_rows(piece):
        return jnp.dot(normed, piece, preferred_element_type=jnp.float32)

    query_proj = add_rows(lax.all_gather(w_query, "ctx", axis=0, tiled=True))
    key_proj = add_rows(lax.all_gather(w_key, "ctx", axis=0, tiled=True))
    value_proj = add_rows(lax.all_gather(w_value, "ctx", axis=0, tiled=True))
    projected = jnp.concatenate([query_proj, key_proj, value_proj], axis=1).astype(jnp.bfloat16)
    taps = short_filter.shape[0]
    previous = shifted(projected[tok_rows - (taps - 1) :], "ctx", 1)
    extended = jnp.concatenate([previous, projected], axis=0).astype(jnp.float32)
    filt_rows = short_filter.reshape(taps, 3 * channels)
    convolved = jnp.zeros((tok_rows, 3 * channels), jnp.float32)
    for tap in range(taps):
        convolved = (
            convolved
            + filt_rows[tap][None, :] * extended[taps - 1 - tap : taps - 1 - tap + tok_rows]
        )
    query_conv = convolved[:, :channels]
    gated = convolved[:, channels : 2 * channels] * convolved[:, 2 * channels :]
    sub_len = math.gcd(tok_rows, 64)
    blocks = tok_rows // sub_len
    lag_index = jnp.arange(sub_len, dtype=jnp.int32)
    lags = lag_index.astype(jnp.float32)
    strength = residue * jnp.sqrt(2.0 * pole_rate)
    kernel = jnp.einsum(
        "lck,ck->lc", jnp.exp(-pole_rate[None] * lags[:, None, None]), strength, precision=highest
    )
    offsets = lag_index[:, None] - lag_index[None, :]
    toeplitz = jnp.where((offsets >= 0)[:, :, None], kernel[jnp.maximum(offsets, 0)], 0.0)
    pieces = gated.reshape(blocks, sub_len, channels)
    inside = jnp.einsum("tsc,bsc->btc", toeplitz, pieces, precision=highest)
    tail_decay = jnp.exp(-pole_rate[None] * (sub_len - 1.0 - lags)[:, None, None])
    block_ends = jnp.einsum("sck,bsc->bck", tail_decay, pieces, precision=highest)
    step_decay = jnp.exp(-pole_rate * float(sub_len))

    def advance(state, block_end):
        return (step_decay * state + block_end, state)

    device_end, entering = lax.scan(advance, jnp.zeros_like(step_decay), block_ends)
    device_decay = jnp.exp(-pole_rate * float(tok_rows))

    def combine(earlier, later):
        return (earlier[0] * later[0], later[0] * earlier[1] + later[1])

    decay_total, incoming = entering_2(
        (device_decay, device_end),
        "ctx",
        combine,
        (jnp.ones_like(device_decay), jnp.zeros_like(device_end)),
    )
    block_pos = jnp.arange(blocks, dtype=jnp.float32) * float(sub_len)
    states_in = entering + jnp.exp(-pole_rate[None] * block_pos[:, None, None]) * incoming[None]
    lead = jnp.exp(-pole_rate[None] * (lags + 1.0)[:, None, None]) * strength[None]
    carried = jnp.einsum("tck,bck->btc", lead, states_in, precision=highest)
    long_conv = (inside + carried).reshape(tok_rows, channels) + skip_gain[None, :] * gated
    mixed = (query_conv * long_conv).astype(jnp.bfloat16)
    all_mixed = lax.all_gather(mixed, "dp", axis=1, tiled=True)
    output = jnp.dot(
        all_mixed,
        lax.all_gather(w_out, "ctx", axis=0, tiled=True),
        preferred_element_type=jnp.float32,
    )
    return (embedded.astype(jnp.float32) + output).astype(jnp.bfloat16)


def remote(src, dst, send, recv, **where):
    return pltpu.make_async_remote_copy(
        src_ref=src,
        dst_ref=dst,
        send_sem=send,
        recv_sem=recv,
        device_id=where,
        device_id_type=MESH,
    )


def greet(ctx_peers, dp_peers):
    barrier = pltpu.get_barrier_semaphore()
    for peer in ctx_peers:
        pl.semaphore_signal(barrier, inc=1, device_id={"ctx": peer}, device_id_type=MESH)
    for peer in dp_peers:
        pl.semaphore_signal(barrier, inc=1, device_id={"dp": peer}, device_id_type=MESH)
    pl.semaphore_wait(barrier, len(ctx_peers) + len(dp_peers))


def flip(index, bit):
    return index + bit - 2 * bit * (lax.rem(index // bit, 2))


def spread_kernel(
    n_ctx,
    n_dp,
    ids_ref,
    gain_ref,
    table_ref,
    wq_ref,
    wk_ref,
    wv_ref,
    ids_out,
    gain_out,
    table_out,
    w_out,
    own_w,
    own_table,
    w_send,
    w_recv,
    id_send,
    id_recv,
    gain_send,
    gain_recv,
    z_send,
    z_recv,
    core_send,
    core_recv,
    local,
):
    me, at = lax.axis_index("ctx"), lax.axis_index("dp")
    depth, wide = wq_ref.shape[0], wq_ref.shape[1] // n_ctx
    vocab = table_ref.shape[0]
    chunks = z_send.shape[2]
    part = vocab // 2 // chunks
    partner = flip(me, 1)
    ctx_peers = [lax.rem(me + d, n_ctx) for d in range(1, n_ctx)]
    dp_peers = [lax.rem(at + d, n_dp) for d in range(1, n_dp)]
    greet(ctx_peers, dp_peers)
    rows = pl.ds(pl.multiple_of(me * depth, depth), depth)
    weights = (wq_ref, wk_ref, wv_ref)

    def half_chunk(core, k):
        return pl.ds(pl.multiple_of((core * chunks + k) * part, part), part)

    def z_copy(source, k, way, hop, peer):
        piece = half_chunk(lax.rem(me, 2), k)
        src = table_ref.at[piece] if hop == 0 else table_out.at[source, piece]
        return remote(
            src,
            table_out.at[source, piece],
            z_send.at[way, hop, k],
            z_recv.at[source, k],
            dp=peer,
        )

    def core_copy(source, core, k):
        piece = half_chunk(core, k)
        return remote(
            table_out.at[source, piece],
            table_out.at[source, piece],
            core_send.at[source, k],
            core_recv.at[source, k],
            ctx=partner,
        )

    for k in range(chunks):

        @pl.when(at < n_dp - 1)
        def _():
            z_copy(at, k, 0, 0, at + 1).start()

        @pl.when(at > 0)
        def _():
            z_copy(at, k, 1, 0, at - 1).start()

    sends = []
    for d, peer in enumerate(ctx_peers):
        copy = remote(ids_ref, ids_out.at[me], id_send.at[d], id_recv.at[me], ctx=peer)
        copy.start()
        sends.append(copy)
    for d, peer in enumerate(dp_peers):
        copy = remote(gain_ref, gain_out.at[at], gain_send.at[d], gain_recv.at[at], dp=peer)
        copy.start()
        sends.append(copy)
    for d, peer in enumerate(ctx_peers):
        for w, weight in enumerate(weights):
            copy = remote(
                weight.at[:, pl.ds(pl.multiple_of(peer * wide, wide), wide)],
                w_out.at[rows, pl.ds(w * wide, wide)],
                w_send.at[d, w],
                w_recv.at[me, w],
                ctx=peer,
            )
            copy.start()
            sends.append(copy)
    into = [
        pltpu.make_async_copy(
            weight.at[:, pl.ds(pl.multiple_of(me * wide, wide), wide)],
            own_w.at[:, pl.ds(w * wide, wide)],
            local.at[w],
        )
        for w, weight in enumerate(weights)
    ]
    into.append(pltpu.make_async_copy(table_ref, own_table, local.at[3]))
    into.append(pltpu.make_async_copy(ids_ref, ids_out.at[me], local.at[4]))
    into.append(pltpu.make_async_copy(gain_ref, gain_out.at[at], local.at[5]))
    for copy in into:
        copy.start()
    for copy in into:
        copy.wait()
    out = [
        pltpu.make_async_copy(own_w, w_out.at[rows], local.at[0]),
        pltpu.make_async_copy(own_table, table_out.at[at], local.at[1]),
    ]
    for copy in out:
        copy.start()

    core = lax.rem(me, 2)
    for hop in range(1, n_dp):
        for k in range(chunks):

            @pl.when(at - hop >= 0)
            def _():
                z_copy(at - hop, k, 0, 0, at).wait_recv()
                core_copy(at - hop, core, k).start()

                if hop < n_dp - 1:

                    @pl.when(at < n_dp - 1)
                    def _():
                        z_copy(at - hop, k, 0, hop, at + 1).start()

            @pl.when(at + hop <= n_dp - 1)
            def _():
                z_copy(at + hop, k, 1, 0, at).wait_recv()
                core_copy(at + hop, core, k).start()

                if hop < n_dp - 1:

                    @pl.when(at > 0)
                    def _():
                        z_copy(at + hop, k, 1, hop, at - 1).start()

    for d in range(1, n_dp):
        source = lax.rem(at + d, n_dp)
        for k in range(chunks):
            core_copy(source, 1 - core, k).wait_recv()
            core_copy(source, core, k).wait_send()
    for hop in range(n_dp - 1):
        for k in range(chunks):

            @pl.when((at - hop >= 0) & (at < n_dp - 1))
            def _():
                z_copy(at - hop, k, 0, hop, at + 1).wait_send()

            @pl.when((at + hop <= n_dp - 1) & (at > 0))
            def _():
                z_copy(at + hop, k, 1, hop, at - 1).wait_send()

    for d, peer in enumerate(ctx_peers):
        remote(ids_ref, ids_out.at[peer], id_send.at[d], id_recv.at[peer], ctx=peer).wait_recv()
        theirs = pl.ds(pl.multiple_of(peer * depth, depth), depth)
        for w, weight in enumerate(weights):
            remote(
                weight.at[:, pl.ds(pl.multiple_of(peer * wide, wide), wide)],
                w_out.at[theirs, pl.ds(w * wide, wide)],
                w_send.at[d, w],
                w_recv.at[peer, w],
                ctx=peer,
            ).wait_recv()
    for d, peer in enumerate(dp_peers):
        remote(gain_ref, gain_out.at[peer], gain_send.at[d], gain_recv.at[peer], dp=peer).wait_recv()
    for copy in sends:
        copy.wait_send()
    for copy in out:
        copy.wait()


def spread(n_ctx, n_dp, ids, gain, table, w_query, w_key, w_value):
    depth, wide = w_query.shape[0], w_query.shape[1] // n_ctx
    chunks = 4
    anywhere = pl.BlockSpec(memory_space=pl.ANY)
    dma = pltpu.SemaphoreType.DMA
    return pl.pallas_call(
        lambda *refs: spread_kernel(n_ctx, n_dp, *refs),
        name="spread",
        out_shape=(
            jax.ShapeDtypeStruct((n_ctx, *ids.shape), ids.dtype),
            jax.ShapeDtypeStruct((n_dp, *gain.shape), gain.dtype),
            jax.ShapeDtypeStruct((n_dp, *table.shape), table.dtype),
            jax.ShapeDtypeStruct((n_ctx * depth, 3 * wide), w_query.dtype),
        ),
        in_specs=[anywhere] * 6,
        out_specs=[anywhere] * 4,
        scratch_shapes=[
            pltpu.VMEM((depth, 3 * wide), w_query.dtype),
            pltpu.VMEM(table.shape, table.dtype),
            dma((n_ctx - 1, 3)),
            dma((n_ctx, 3)),
            dma((n_ctx - 1,)),
            dma((n_ctx,)),
            dma((n_dp - 1,)),
            dma((n_dp,)),
            dma((2, n_dp - 1, chunks)),
            dma((n_dp, chunks)),
            dma((n_dp, chunks)),
            dma((n_dp, chunks)),
            dma((6,)),
        ],
        compiler_params=pltpu.CompilerParams(
            collective_id=0, has_side_effects=True, vmem_limit_bytes=53 << 20
        ),
    )(ids, gain, table, w_query, w_key, w_value)


def mix_kernel(
    me_ref,
    ids_ref,
    gain_ref,
    table_ref,
    w_ref,
    filt_ref,
    rate_ref,
    residue_ref,
    skip_ref,
    out_ref,
    proj,
    gated,
    query,
):
    n_dp, vocab, width = table_ref.shape
    features = n_dp * width
    taps = filt_ref.shape[0]
    modes = rate_ref.shape[1]
    segments, steps, lanes = out_ref.shape
    lead = proj.shape[1] - segments * steps
    mine = pl.ds(pl.multiple_of(me_ref[0] * lanes, lanes), lanes)
    total = jnp.zeros((vocab, 1), jnp.float32)
    for b in range(n_dp):
        block = table_ref[b].astype(jnp.float32)
        total = total + jnp.sum(block * block, axis=1, keepdims=True)
    scale = lax.rsqrt(total / features + 1e-06)
    rows = jnp.zeros((vocab, 3 * lanes), jnp.float32)
    for b in range(n_dp):
        block = table_ref[b].astype(jnp.float32)
        gain = jnp.concatenate([gain_ref[b, r : r + 1, :] for r in range(width // lanes)], axis=1)
        normed = (block * scale * gain).astype(jnp.bfloat16)
        rows = rows + jnp.dot(
            normed, w_ref[b * width : (b + 1) * width, :], preferred_element_type=jnp.float32
        )
    rows = rows.astype(jnp.bfloat16)
    pieces = steps // lanes
    per_segment = ids_ref.shape[1]
    names = lax.broadcasted_iota(jnp.int32, (lanes, vocab), 1)
    for s in range(segments):
        by_lane = ids_ref[s].astype(jnp.float32)
        square = jnp.concatenate(
            [by_lane, jnp.zeros((lanes - per_segment, lanes), jnp.float32)], axis=0
        )
        columns = square.T.astype(jnp.int32)
        one_hot = jnp.concatenate(
            [
                (columns[:, p : p + 1] == names).astype(jnp.float32).astype(jnp.bfloat16)
                for p in range(pieces)
            ],
            axis=0,
        )
        picked = jnp.dot(one_hot, rows, preferred_element_type=jnp.float32)
        for w in range(3):
            proj[w, pl.ds(lead + s, steps, stride=segments), :] = picked[:, w * lanes : (w + 1) * lanes]
    place_of = lax.broadcasted_iota(jnp.int32, (segments, lanes), 0)

    def later(value, by):
        return jnp.where(place_of >= by, pltpu.roll(value, by, 0), 0.0)

    end = proj.shape[1]
    for tap in range(1, taps):
        for w in range(3):
            tail = proj[w, end - tap * segments : end - (tap - 1) * segments, :]
            proj[w, lead - tap * segments : lead - (tap - 1) * segments, :] = later(tail, 1)
    size = lanes

    def convolve(n, carry):
        start = n * size + lead
        conv = [jnp.zeros((size, lanes), jnp.float32) for _ in range(3)]
        for tap in range(taps):
            here = pl.ds(pl.multiple_of(start - tap * segments, segments), size)
            for w in range(3):
                conv[w] = conv[w] + filt_ref[tap, w : w + 1, mine] * proj[w, here, :]
        there = pl.ds(pl.multiple_of(n * size, size), size)
        query[there, :] = conv[0]
        gated[there, :] = conv[1] * conv[2]
        return carry

    lax.fori_loop(0, segments * steps // size, convolve, 0)

    def spread_rows(row):
        return jnp.broadcast_to(row, (segments, lanes))

    def turned(ref):
        value = ref[mine, :]
        return jnp.concatenate([value, jnp.zeros((lanes, lanes - modes), jnp.float32)], axis=1).T

    rate, residue = turned(rate_ref), turned(residue_ref)
    decay = [spread_rows(jnp.exp(-rate[m : m + 1, :])) for m in range(modes)]
    unroll = 4

    def ends(n, state):
        for u in range(unroll):
            row = gated[pl.ds(pl.multiple_of((n * unroll + u) * segments, segments), segments), :]
            state = tuple(d * s + row for d, s in zip(decay, state))
        return state

    zero = jnp.zeros((segments, lanes), jnp.float32)
    state = lax.fori_loop(0, steps // unroll, ends, (zero,) * modes)
    entering = []
    for m in range(modes):
        value = later(state[m], 1)
        by = 1
        while by < segments:
            jump = jnp.exp(-rate[m : m + 1, :] * float(steps * by))
            value = value + jump * later(value, by)
            by *= 2
        entering.append(value)
    strength = [
        spread_rows(residue[m : m + 1, :] * jnp.sqrt(2.0 * rate[m : m + 1, :])) for m in range(modes)
    ]
    skip = spread_rows(skip_ref[:, mine])

    def advance(n, state):
        for u in range(unroll):
            here = pl.ds(pl.multiple_of((n * unroll + u) * segments, segments), segments)
            row = gated[here, :]
            sums = [skip * row, None]
            new = []
            for m in range(modes):
                now = decay[m] * state[m] + row
                new.append(now)
                term = strength[m] * now
                sums[m % 2] = term if sums[m % 2] is None else sums[m % 2] + term
            state = tuple(new)
            query[here, :] = query[here, :] * (sums[0] + sums[1])
        return state

    lax.fori_loop(0, steps // unroll, advance, tuple(entering))
    for s in range(segments):
        out_ref[s] = query[pl.ds(s, steps, stride=segments), :].astype(jnp.bfloat16)


def mix(me, ids, gain, table, w, filt, rate, residue, skip, segments, steps):
    whole = pl.BlockSpec(memory_space=pltpu.VMEM)
    lanes = w.shape[1] // 3
    lead = segments * (filt.shape[0] - 1)
    return pl.pallas_call(
        mix_kernel,
        name="mix",
        out_shape=jax.ShapeDtypeStruct((segments, steps, lanes), jnp.bfloat16),
        in_specs=[pl.BlockSpec(memory_space=pltpu.SMEM)] + [whole] * 8,
        out_specs=whole,
        scratch_shapes=[
            pltpu.VMEM((3, lead + segments * steps, lanes), jnp.float32),
            pltpu.VMEM((segments * steps, lanes), jnp.float32),
            pltpu.VMEM((segments * steps, lanes), jnp.float32),
        ],
        compiler_params=pltpu.CompilerParams(vmem_limit_bytes=VMEM_BYTES),
    )(me, ids, gain, table, w, filt, rate, residue, skip)


def collect_kernel(
    n_ctx,
    n_dp,
    mixed_ref,
    weight_ref,
    mixed_out,
    weight_out,
    own_mixed,
    own_weight,
    a_send,
    slot_recv,
    z_send,
    w_send,
    w_recv,
    core_send,
    core_recv,
    local,
):
    me, at = lax.axis_index("ctx"), lax.axis_index("dp")
    depth, lanes = weight_ref.shape[0], mixed_ref.shape[2]
    bits = [1 << b for b in range(n_ctx.bit_length() - 1)]
    ctx_peers = [lax.rem(me + d, n_ctx) for d in range(1, n_ctx)]
    near = [(at - 1, at > 0), (at + 1, at < n_dp - 1)]
    barrier = pltpu.get_barrier_semaphore()
    dp_peers = [lax.rem(at + d, n_dp) for d in range(1, n_dp)]
    greet(ctx_peers, dp_peers)
    partner, side, up = flip(me, 1), flip(me, 2), flip(me, 4)
    across = flip(side, 4)
    half = depth // 2

    def slot(source, k):
        start = (source * n_ctx + k) * lanes
        return mixed_out.at[:, pl.ds(pl.multiple_of(start, lanes), lanes)]

    def turn(d, peer):
        return remote(mixed_ref.at[peer], slot(at, me), a_send.at[d - 1], slot_recv.at[at, me], ctx=peer)

    def block(owner, first=0, count=None):
        count = depth if count is None else count
        start = pl.multiple_of(owner * depth + first, half)
        return weight_out.at[pl.ds(start, count)]

    for d, peer in enumerate(ctx_peers):
        turn(d + 1, peer).start()
    into = [
        pltpu.make_async_copy(mixed_ref.at[me], own_mixed, local.at[0]),
        pltpu.make_async_copy(weight_ref, own_weight, local.at[1]),
    ]
    for copy in into:
        copy.start()

    def z_copy(source, d, way, hop, peer):
        k = lax.rem(me + d, n_ctx)
        src = mixed_ref.at[me] if hop == 0 and d == 0 else slot(source, k)
        return remote(src, slot(source, k), z_send.at[way, hop, d], slot_recv.at[source, k], dp=peer)

    def recv(source, d):
        k = lax.rem(me + d, n_ctx)
        z_copy_like = remote(slot(source, k), slot(source, k), z_send.at[0, 0, d], slot_recv.at[source, k], ctx=partner)
        z_copy_like.wait_recv()

    def first_hop(d):
        @pl.when(at < n_dp - 1)
        def _():
            z_copy(at, d, 0, 0, at + 1).start()

        @pl.when(at > 0)
        def _():
            z_copy(at, d, 1, 0, at - 1).start()

    first_hop(0)
    own = [
        remote(weight_ref, block(me), w_send.at[0], w_recv.at[0], ctx=side),
        remote(weight_ref, block(me), w_send.at[1], w_recv.at[1], ctx=up),
        remote(weight_ref, block(me), w_send.at[2], w_recv.at[2], ctx=partner),
    ]
    own[2].start()
    for copy in into:
        copy.wait()
    out = [
        pltpu.make_async_copy(own_mixed, slot(at, me), local.at[0]),
        pltpu.make_async_copy(own_weight, block(me), local.at[1]),
    ]
    for copy in out:
        copy.start()
    for d in range(1, n_ctx):
        recv(at, d)
        first_hop(d)
    own[0].start()
    own[1].start()

    for hop in range(1, n_dp):
        for d in range(n_ctx):

            @pl.when(at - hop >= 0)
            def _():
                recv(at - hop, d)

                if hop < n_dp - 1:

                    @pl.when(at < n_dp - 1)
                    def _():
                        z_copy(at - hop, d, 0, hop, at + 1).start()

            @pl.when(at + hop <= n_dp - 1)
            def _():
                recv(at + hop, d)

                if hop < n_dp - 1:

                    @pl.when(at > 0)
                    def _():
                        z_copy(at + hop, d, 1, hop, at - 1).start()

        if hop == 1:
            own[0].wait_recv()
            own[1].wait_recv()
            passed = [
                remote(block(side, 0, half), block(side, 0, half), w_send.at[3], w_recv.at[3], ctx=up),
                remote(block(up, half, half), block(up, half, half), w_send.at[4], w_recv.at[4], ctx=side),
                remote(block(side), block(side), core_send.at[0], core_recv.at[0], ctx=partner),
                remote(block(up), block(up), core_send.at[1], core_recv.at[1], ctx=partner),
            ]
            for copy in passed:
                copy.start()
    passed[0].wait_recv()
    passed[1].wait_recv()
    last = [
        remote(block(across, 0, half), block(across, 0, half), core_send.at[2], core_recv.at[2], ctx=partner),
        remote(block(across, half, half), block(across, half, half), core_send.at[3], core_recv.at[3], ctx=partner),
    ]
    for copy in last:
        copy.start()
    own[2].wait_recv()
    passed[2].wait_recv()
    passed[3].wait_recv()
    for copy in last:
        copy.wait_recv()
    for copy in own + passed + last:
        copy.wait_send()
    for d, peer in enumerate(ctx_peers):
        turn(d + 1, peer).wait_send()
    for hop in range(n_dp - 1):
        for d in range(n_ctx):

            @pl.when((at - hop >= 0) & (at < n_dp - 1))
            def _():
                z_copy(at - hop, d, 0, hop, at + 1).wait_send()

            @pl.when((at + hop <= n_dp - 1) & (at > 0))
            def _():
                z_copy(at + hop, d, 1, hop, at - 1).wait_send()

    for copy in out:
        copy.wait()


def collect(n_ctx, n_dp, mixed, weight):
    depth, columns = weight.shape
    steps, lanes = mixed.shape[1:]
    anywhere = pl.BlockSpec(memory_space=pl.ANY)
    dma = pltpu.SemaphoreType.DMA
    return pl.pallas_call(
        lambda *refs: collect_kernel(n_ctx, n_dp, *refs),
        name="collect",
        out_shape=(
            jax.ShapeDtypeStruct((steps, n_dp * n_ctx * lanes), mixed.dtype),
            jax.ShapeDtypeStruct((n_ctx * depth, columns), weight.dtype),
        ),
        in_specs=[anywhere] * 2,
        out_specs=[anywhere] * 2,
        scratch_shapes=[
            pltpu.VMEM((steps, lanes), mixed.dtype),
            pltpu.VMEM((depth, columns), weight.dtype),
            dma((n_ctx - 1,)),
            dma((n_dp, n_ctx)),
            dma((2, n_dp - 1, n_ctx)),
            dma((5,)),
            dma((5,)),
            dma((4,)),
            dma((4,)),
            dma((2,)),
        ],
        compiler_params=pltpu.CompilerParams(
            collective_id=1, has_side_effects=True, vmem_limit_bytes=8 << 20
        ),
    )(mixed, weight)


def by_channel(
    n_ctx,
    n_dp,
    ids,
    embed_table,
    norm_gain,
    w_query,
    w_key,
    w_value,
    short_filter,
    pole_rate,
    residue,
    skip_gain,
    w_out,
):
    vocab = embed_table.shape[0]
    tok_rows = ids.shape[0]
    gain = norm_gain.astype(jnp.float32).reshape(-1, LANES)
    by_lane = ids.reshape(-1, LANES)
    by_lane = jnp.pad(by_lane, ((0, -by_lane.shape[0] % SUBLANES), (0, 0)))
    all_ids, all_gain, all_table, w_mine = spread(
        n_ctx, n_dp, by_lane, gain, embed_table, w_query, w_key, w_value
    )
    mixed = mix(
        lax.axis_index("ctx").astype(jnp.int32).reshape(1),
        all_ids,
        all_gain,
        all_table,
        w_mine,
        short_filter,
        pole_rate,
        residue,
        skip_gain[None, :],
        n_ctx,
        tok_rows,
    )
    all_mixed, all_rows = collect(n_ctx, n_dp, mixed, w_out)
    one_hot = (ids[:, None] == jnp.arange(vocab, dtype=jnp.int32)[None, :]).astype(jnp.bfloat16)
    embedded = jnp.dot(one_hot, embed_table, preferred_element_type=jnp.float32)
    output = jnp.dot(all_mixed, all_rows, preferred_element_type=jnp.float32)
    return (embedded + output).astype(jnp.bfloat16)


def solution(mesh):
    placed = (
        P("ctx"),
        P(None, "dp"),
        P("dp"),
        P("ctx", "dp"),
        P("ctx", "dp"),
        P("ctx", "dp"),
        P(None, None, "dp"),
        P("dp", None),
        P("dp", None),
        P("dp"),
        P("ctx", "dp"),
    )
    n_ctx, n_dp = mesh.shape["ctx"], mesh.shape["dp"]

    def body(*args):
        ids, w_query = args[0], args[3]
        fits = (
            n_ctx == SUBLANES
            and n_dp > 1
            and w_query.shape[1] == n_ctx * LANES
            and ids.shape[0] % LANES == 0
        )
        if fits:
            return by_channel(n_ctx, n_dp, *args)
        return shards(*args)

    return jax.shard_map(
        body, mesh=mesh, in_specs=placed, out_specs=P("ctx", "dp"), check_vma=False
    )
```
